128 devices in a mesh: row: 8 (over y, z_hi), col: 16 (over x, z_lo, core).
Axes of the slice: x: 4, y: 4, z: 4 (z_hi: 2, z_lo: 2; z = z_hi * 2 + z_lo), core: 2. Of those that a mesh axis runs over, the one named last changes fastest.
Arguments:
- voltages: bfloat16 [2, 64, 64, 2, 31744], P(None, 'row', 'col'), may hold values from -6 to 6
- fir: float32 [16, 1024], replicated, may hold values from -0.046875 to 0.046875
Outputs:
- power: float32 [64, 64, 2, 1024], P('col', None, None, 'row')
The draws below stay inside these ranges and needn't reach their ends.
All inputs are finite; a program needn't handle non-finite values.
Results may differ from the reference program's by a relative error of at most 0.0032.
Values may be sent and summed in bfloat16 or wider, within the bound.
No kernel may reach another device: no remote copies, remote signals or barrier semaphores. Data moves between devices by JAX's collectives and lax.ppermute only.
A program may use at most 192 MiB of HBM per device.

```python
import math
import jax
import jax.numpy as jnp
from jax import lax

NROW = 64
NCOL = 64
POL = 2
NCHAN = 1024
TAPS = 16
FRAMES = 16
SAMPLES = 31744


def shard_levels(rng, extent, cuts, smallest, high):
    gain = 1.0
    for dim, parts in cuts:
        steps = jax.random.uniform(jax.random.fold_in(jax.random.fold_in(rng, 6), dim), (parts,), jnp.float32, smallest / len(cuts), high / len(cuts))
        gain = gain * jnp.repeat(jnp.exp(steps), extent[dim] // parts).reshape((-1,) + (1,) * (len(extent) - 1 - dim))
    return gain


def bell_draw(key, dims, scale, limit, split=(), kind=jnp.bfloat16):
    values = jax.random.normal(key, dims, jnp.float32) * scale
    if len(split) > 0:
        values = shard_levels(key, dims, split, -0.22, 0.18) * values
    return jnp.clip(values, min=-limit, max=limit).astype(kind)


def setup_inputs(seed: int = 0) -> dict:
    keys = jax.random.split(jax.random.key(seed), 3)
    return {
        "voltages": bell_draw(keys[0], (2, NROW, NCOL, POL, SAMPLES), 1.0, 6.0, ((1, 8), (2, 16))),
        "fir": bell_draw(keys[1], (TAPS, NCHAN), (TAPS * NCHAN) ** -0.5, 0.046875, (), jnp.float32),
    }


def spatial_table(length):
    index = jnp.arange(length, dtype=jnp.int32)
    angle = ((index[:, None] * index[None, :]) % length).astype(jnp.float32) * (2.0 * math.pi / length)
    cosine = jnp.cos(angle).astype(jnp.bfloat16)
    sine = jnp.sin(angle).astype(jnp.bfloat16)
    return jnp.stack([jnp.stack([cosine, -sine]), jnp.stack([sine, cosine])])


def channelize_row(volt_row, fir):
    shaped = volt_row.reshape(2, NCOL, POL, FRAMES + TAPS - 1, NCHAN)
    filtered = jnp.zeros((2, NCOL, POL, FRAMES, NCHAN), jnp.float32)
    for tap in range(TAPS):
        filtered = filtered + shaped[:, :, :, tap:tap + FRAMES, :].astype(jnp.float32) * fir[tap]
    spectrum = jnp.fft.fft(lax.complex(filtered[0], filtered[1]), axis=-1)
    return jnp.stack([jnp.real(spectrum), jnp.imag(spectrum)]).astype(jnp.bfloat16)


def reference(voltages, fir):
    by_row = jnp.moveaxis(voltages, 1, 0)
    spectra = lax.map(lambda volt_row: channelize_row(volt_row, fir), by_row)
    per_frame = jnp.moveaxis(spectra, 4, 0)
    row_tab = spatial_table(NROW).astype(jnp.float32)
    col_tab = spatial_table(NCOL).astype(jnp.float32)

    def frame_step(total, frame_data):
        rowbeam = jnp.einsum("xcbpk,cdux->dubpk", frame_data.astype(jnp.float32), row_tab).astype(jnp.bfloat16)
        beams = jnp.einsum("cubpk,cdvb->duvpk", rowbeam.astype(jnp.float32), col_tab)
        return total + jnp.sum(beams * beams, axis=0), None

    start = jnp.zeros((NROW, NCOL, POL, NCHAN), jnp.float32)
    total, _ = lax.scan(frame_step, start, per_frame)
    return total * (1.0 / (FRAMES * NROW * NCOL))
```

```python
import functools

import jax
import jax.numpy as jnp
import numpy as np
from jax import lax
from jax.experimental import pallas as pl
from jax.experimental.pallas import tpu as pltpu
from jax.sharding import PartitionSpec as P

NROW = 64
NCOL = 64
POL = 2
NCHAN = 1024
TAPS = 16
FRAMES = 16
ROWS = 8
COLS = 16
A = NROW // ROWS
B = NCOL // COLS
BLOCKS = FRAMES + TAPS - 1
LANES = 128
F32 = jnp.float32
BF16 = jnp.bfloat16


def bf16_pair(angle):
    cosine = np.cos(angle).astype(np.float32).astype(jnp.bfloat16)
    sine = np.sin(angle).astype(np.float32).astype(jnp.bfloat16)
    return cosine, sine


def complex_table(angle):
    cosine, sine = bf16_pair(angle)
    real = np.stack([cosine, sine], axis=-1)
    imag = np.stack([-sine, cosine], axis=-1)
    return np.stack([real, imag], axis=1)


def dft_table():
    k = np.arange(256)
    table = complex_table(2.0 * np.pi * (np.outer(k, k) % 256) / 256)
    return table.transpose(0, 1, 3, 2).reshape(512, 512)


def twiddle_table():
    n = np.arange(256)
    angle = 2.0 * np.pi * np.outer(np.arange(4), n) / NCHAN
    return np.concatenate([np.cos(angle), np.sin(angle)]).astype(np.float32)


def spatial(length):
    index = np.arange(length)
    return complex_table(2.0 * np.pi * (np.outer(index, index) % length) / length)


def row_matrix():
    table = spatial(NROW).reshape(NROW, 2, ROWS, A, 2)
    return table.transpose(0, 1, 2, 4, 3).reshape(2 * NROW, 2 * NROW)


def col_matrix():
    return spatial(NCOL).transpose(1, 0, 3, 2).reshape(2 * NCOL, 2 * NCOL)


def sum_matrix():
    eye = np.eye(8, dtype=np.float32).reshape(2, 4, 2, 4)
    full = np.einsum("hqHQ,pP,f->phqHQPf", eye, np.eye(2, dtype=np.float32), np.ones(FRAMES, np.float32))
    return (full.reshape(16, 256) / (FRAMES * NROW * NCOL)).astype(jnp.bfloat16)


def channelize_kernel(x_ref, fir_ref, dft_ref, tw_ref, out_ref, coef, filt, zed, turn):
    @pl.when(pl.program_id(0) == 0)
    def _():
        for s in range(8):
            piece = fir_ref[:, s * LANES:(s + 1) * LANES]
            for p in range(POL):
                coef[pl.ds(2 * s + p, TAPS, stride=16), :] = piece

    def filter_one(unit, carry):
        half = unit % 2
        part = (unit // 2) % 2
        which = unit // 4
        ant = 2 * carry + which
        taps = [coef[pl.ds(pl.multiple_of(16 * t + 8 * half, 8), 8), :] for t in range(TAPS)]
        xs = [
            x_ref[part, ant, 0, pl.ds(pl.multiple_of(16 * i + 8 * half, 8), 8), :].astype(F32)
            for i in range(BLOCKS)
        ]
        for f in range(FRAMES):
            terms = [taps[t] * xs[f + t] for t in range(TAPS)]
            while len(terms) > 1:
                terms = [a + b for a, b in zip(terms[::2], terms[1::2])]
            filt[which, part, pl.ds(pl.multiple_of(16 * f + 8 * half, 8), 8), :] = terms[0]
        return carry

    def pair_step(pair, carry):
        lax.fori_loop(0, 8, filter_one, pair)
        for which in range(2):
            for p in range(POL):
                for lo in range(2):
                    re = []
                    im = []
                    for j in range(4):
                        row = 2 * (2 * j + lo) + p
                        re.append(filt[which, 0, pl.ds(row, FRAMES, stride=16), :])
                        im.append(filt[which, 1, pl.ds(row, FRAMES, stride=16), :])
                    sr0, si0 = re[0] + re[2], im[0] + im[2]
                    sr1, si1 = re[1] + re[3], im[1] + im[3]
                    dr0, di0 = re[0] - re[2], im[0] - im[2]
                    dr1, di1 = re[1] - re[3], im[1] - im[3]
                    outs = [
                        (sr0 + sr1, si0 + si1),
                        (dr0 + di1, di0 - dr1),
                        (sr0 - sr1, si0 - si1),
                        (dr0 - di1, di0 + dr1),
                    ]
                    for q in range(4):
                        zr, zi = outs[q]
                        if q > 0:
                            cosine = tw_ref[q:q + 1, lo * LANES:(lo + 1) * LANES]
                            sine = tw_ref[4 + q:5 + q, lo * LANES:(lo + 1) * LANES]
                            zr, zi = zr * cosine + zi * sine, zi * cosine - zr * sine
                        r0 = which * LANES + q * 32 + p * 16
                        zed[r0:r0 + 16, lo * LANES:(lo + 1) * LANES] = zr.astype(BF16)
                        zed[r0:r0 + 16, (2 + lo) * LANES:(3 + lo) * LANES] = zi.astype(BF16)
        spec = lax.dot_general(
            dft_ref[...], zed[...], (((1,), (1,)), ((), ())), preferred_element_type=F32
        )
        for which in range(2):
            turn[pl.ds(2 * pair + which, 512, stride=A), :] = spec[:, which * LANES:(which + 1) * LANES]
        return carry

    lax.fori_loop(0, A // 2, pair_step, 0)
    out_ref[:, 0] = turn[...].reshape(128, 2, 16, LANES).astype(BF16)


def channelize(volts, fir):
    flat = volts.reshape(2, A, B, POL, BLOCKS * 8, LANES)
    flat = flat.swapaxes(3, 4).reshape(2, A, B, BLOCKS * 16, LANES)
    return pl.pallas_call(
        channelize_kernel,
        name="channelize",
        grid=(B,),
        in_specs=[
            pl.BlockSpec((2, A, 1, BLOCKS * 16, LANES), lambda b: (0, 0, b, 0, 0)),
            pl.BlockSpec((TAPS, NCHAN), lambda b: (0, 0)),
            pl.BlockSpec((512, 512), lambda b: (0, 0)),
            pl.BlockSpec((8, 256), lambda b: (0, 0)),
        ],
        out_specs=pl.BlockSpec((128, 1, 2, 16, LANES), lambda b: (0, b, 0, 0, 0)),
        out_shape=jax.ShapeDtypeStruct((128, B, 2, 16, LANES), BF16),
        scratch_shapes=[
            pltpu.VMEM((TAPS * 16, LANES), F32),
            pltpu.VMEM((2, 2, FRAMES * 16, LANES), F32),
            pltpu.VMEM((256, 512), BF16),
            pltpu.VMEM((512 * A, LANES), F32),
        ],
        compiler_params=pltpu.CompilerParams(vmem_limit_bytes=40 << 20),
    )(flat, fir, jnp.asarray(dft_table()), jnp.asarray(twiddle_table()))


def beam_kernel(in_ref, row_ref, col_ref, sum_ref, out_ref, turn):
    step = pl.program_id(0)

    def row_step(i, carry):
        b4 = i % B
        col = i // B
        b = i
        for h in range(2):
            piece = in_ref[:, col, b4, h].reshape(128, LANES)
            got = jnp.dot(row_ref[...], piece, preferred_element_type=F32)
            turn[h, pl.ds(b, 128, stride=NCOL), :] = got
        return carry

    lax.fori_loop(0, NCOL, row_step, 0)

    def col_step(g, carry):
        pows = []
        for j in range(4):
            base = pl.multiple_of((4 * g + j) * 128, 128)
            halves = []
            for h in range(2):
                mid = turn[h, pl.ds(base, 128), :].astype(BF16)
                beam = jnp.dot(col_ref[...], mid, preferred_element_type=F32)
                re = beam[:NCOL]
                im = beam[NCOL:]
                halves.append((re * re + im * im).astype(BF16))
            pows.append(jnp.concatenate(halves, axis=1))
        power = jnp.concatenate(pows, axis=0)
        out_ref[g] = lax.dot_general(
            sum_ref[...], power, (((1,), (1,)), ((), ())), preferred_element_type=F32
        )
        return carry

    lax.fori_loop(0, COLS, col_step, 0)


def beamform(got):
    return pl.pallas_call(
        beam_kernel,
        name="beamform",
        grid=(1,),
        in_specs=[
            pl.BlockSpec((ROWS, COLS, B, 2, 16, LANES), lambda i: (0, 0, 0, 0, 0, 0)),
            pl.BlockSpec((128, 128), lambda i: (0, 0)),
            pl.BlockSpec((128, 128), lambda i: (0, 0)),
            pl.BlockSpec((16, 256), lambda i: (0, 0)),
        ],
        out_specs=pl.BlockSpec((COLS, 16, 256), lambda i: (0, 0, 0)),
        out_shape=jax.ShapeDtypeStruct((COLS, 16, 256), F32),
        scratch_shapes=[pltpu.VMEM((2, 128 * NCOL, LANES), F32)],
        compiler_params=pltpu.CompilerParams(vmem_limit_bytes=40 << 20),
    )(
        got.reshape(ROWS, COLS, B, 2, 16, LANES),
        jnp.asarray(row_matrix()),
        jnp.asarray(col_matrix()),
        jnp.asarray(sum_matrix()),
    )


def finish_kernel(in_ref, out_ref):
    for p in range(POL):
        piece = in_ref[:, p * 8:(p + 1) * 8, :].reshape(128, 256)
        out_ref[pl.ds(p, 256, stride=2), :] = piece.T


def finish(got):
    return pl.pallas_call(
        finish_kernel,
        name="finish",
        out_shape=jax.ShapeDtypeStruct((256 * POL, LANES), F32),
    )(got)


def body(volts, fir):
    spectra = channelize(volts, fir)
    gathered = lax.all_to_all(spectra, ("row", "col"), 0, 0, tiled=True)
    partial = beamform(gathered)
    swapped = lax.all_to_all(partial, "col", 0, 0, tiled=True)
    return finish(swapped).reshape(NROW // COLS, NCOL, POL, LANES)


def solution(mesh):
    in_specs = (P(None, "row", "col", None, None), P())
    out_specs = P("col", None, None, "row")
    return jax.shard_map(body, mesh=mesh, in_specs=in_specs, out_specs=out_specs, check_vma=False)
```

```python
import functools

import jax
import jax.numpy as jnp
import numpy as np
from jax import lax
from jax.experimental import pallas as pl
from jax.experimental.pallas import tpu as pltpu
from jax.sharding import PartitionSpec as P

NROW = 64
NCOL = 64
POL = 2
NCHAN = 1024
TAPS = 16
FRAMES = 16
ROWS = 8
COLS = 16
A = NROW // ROWS
B = NCOL // COLS
BLOCKS = FRAMES + TAPS - 1
LANES = 128
GROUP = 4
F32 = jnp.float32
BF16 = jnp.bfloat16


def bf16_pair(angle):
    cosine = np.cos(angle).astype(np.float32).astype(jnp.bfloat16)
    sine = np.sin(angle).astype(np.float32).astype(jnp.bfloat16)
    return cosine, sine


def complex_table(angle):
    cosine, sine = bf16_pair(angle)
    real = np.stack([cosine, sine], axis=-1)
    imag = np.stack([-sine, cosine], axis=-1)
    return np.stack([real, imag], axis=1)


def dft_table():
    k = np.arange(256)
    table = complex_table(2.0 * np.pi * (np.outer(k, k) % 256) / 256)
    return table.transpose(0, 1, 3, 2).reshape(512, 512)


def twiddle_table():
    n = np.arange(256)
    angle = 2.0 * np.pi * np.outer(np.arange(4), n) / NCHAN
    return np.concatenate([np.cos(angle), np.sin(angle)]).astype(np.float32)


def spatial(length):
    index = np.arange(length)
    return complex_table(2.0 * np.pi * (np.outer(index, index) % length) / length)


def row_matrix():
    table = spatial(NROW).reshape(NROW, 2, ROWS, A, 2)
    return table.transpose(0, 1, 2, 4, 3).reshape(2 * NROW, 2 * NROW)


def col_matrix():
    table = spatial(NCOL).reshape(NCOL, 2, 8, 8, 2)
    return table.transpose(1, 0, 2, 4, 3).reshape(2 * NCOL, 2 * NCOL)


def sum_matrix():
    eye = np.eye(8, dtype=np.float32).reshape(2, 4, 2, 4)
    full = np.einsum("hqHQ,pP,f->phqHQPf", eye, np.eye(2, dtype=np.float32), np.ones(FRAMES, np.float32))
    return (full.reshape(16, 256) / (FRAMES * NROW * NCOL)).astype(jnp.bfloat16)


def channelize_kernel(x_hbm, fir_hbm, dft_hbm, tw_hbm, out_ref, x_ref, fir_ref, dft_ref, tw_ref, coef, filt, zed, turn, sems):
    x_copies = [pltpu.make_async_copy(x_hbm.at[:, :, b], x_ref.at[b], sems.at[b]) for b in range(B)]
    fir_copy = pltpu.make_async_copy(fir_hbm, fir_ref, sems.at[B])
    dft_copy = pltpu.make_async_copy(dft_hbm, dft_ref, sems.at[B + 1])
    tw_copy = pltpu.make_async_copy(tw_hbm, tw_ref, sems.at[B + 2])
    fir_copy.start()
    x_copies[0].start()
    tw_copy.start()
    dft_copy.start()
    for b in range(1, B):
        x_copies[b].start()
    fir_copy.wait()
    for s in range(8):
        piece = fir_ref[:, s * LANES:(s + 1) * LANES]
        for p in range(POL):
            coef[pl.ds(2 * s + p, TAPS, stride=16), :] = piece

    def filter_pair(index):
        col = index // (A // 2)
        pair = index % (A // 2)
        for which in range(2):
            for part in range(2):
                taps = [coef[16 * t:16 * t + 16, :].astype(BF16) for t in range(TAPS)]
                xs = [x_ref[col, part, 2 * pair + which, 16 * i:16 * i + 16, :] for i in range(BLOCKS)]
                for f in range(FRAMES):
                    terms = [taps[t] * xs[f + t] for t in range(TAPS)]
                    while len(terms) > TAPS // GROUP:
                        terms = [a + b for a, b in zip(terms[::2], terms[1::2])]
                    terms = [t.astype(F32) for t in terms]
                    while len(terms) > 1:
                        terms = [a + b for a, b in zip(terms[::2], terms[1::2])]
                    row = (f // 8) * 128 + f % 8
                    filt[which, part, pl.ds(row, 16, stride=8), :] = terms[0]

    def load_rows(which, part, row):
        lo = filt[which, part, row * 8:row * 8 + 8, :]
        hi = filt[which, part, 128 + row * 8:128 + row * 8 + 8, :]
        return jnp.concatenate([lo, hi], axis=0)

    def butterfly():
        for which in range(2):
            for p in range(POL):
                for lo in range(2):
                    rows = [2 * (2 * j + lo) + p for j in range(4)]
                    re = [load_rows(which, 0, row) for row in rows]
                    im = [load_rows(which, 1, row) for row in rows]
                    sr0, si0 = re[0] + re[2], im[0] + im[2]
                    sr1, si1 = re[1] + re[3], im[1] + im[3]
                    dr0, di0 = re[0] - re[2], im[0] - im[2]
                    dr1, di1 = re[1] - re[3], im[1] - im[3]
                    outs = [
                        (sr0 + sr1, si0 + si1),
                        (dr0 + di1, di0 - dr1),
                        (sr0 - sr1, si0 - si1),
                        (dr0 - di1, di0 + dr1),
                    ]
                    for q in range(4):
                        zr, zi = outs[q]
                        if q > 0:
                            cosine = tw_ref[q:q + 1, lo * LANES:(lo + 1) * LANES]
                            sine = tw_ref[4 + q:5 + q, lo * LANES:(lo + 1) * LANES]
                            zr, zi = zr * cosine + zi * sine, zi * cosine - zr * sine
                        r0 = which * LANES + q * 32 + p * 16
                        zed[r0:r0 + 16, lo * LANES:(lo + 1) * LANES] = zr.astype(BF16)
                        zed[r0:r0 + 16, (2 + lo) * LANES:(3 + lo) * LANES] = zi.astype(BF16)

    x_copies[0].wait()
    filter_pair(0)
    tw_copy.wait()
    dft_copy.wait()

    def col_step(col, carry):
        @pl.when(col < B - 1)
        def _():
            pltpu.make_async_copy(x_hbm.at[:, :, col + 1], x_ref.at[col + 1], sems.at[col + 1]).wait()

        def pair_step(pair, carry):
            butterfly()
            filter_pair(jnp.minimum(col * (A // 2) + pair + 1, B * A // 2 - 1))
            spec = lax.dot_general(
                dft_ref[...], zed[...], (((1,), (1,)), ((), ())), preferred_element_type=F32
            )
            for which in range(2):
                turn[pl.ds(2 * pair + which, 512, stride=A), :] = spec[:, which * LANES:(which + 1) * LANES]
            return carry

        lax.fori_loop(0, A // 2, pair_step, 0)
        out_ref[:, col] = turn[...].reshape(128, 2, 16, LANES).astype(BF16)
        return carry

    lax.fori_loop(0, B, col_step, 0)


def in_hbm(x):
    return pltpu.with_memory_space_constraint(x, pltpu.HBM)


def channelize(volts, fir):
    flat = volts.reshape(2, A, B, POL, BLOCKS * 8, LANES)
    flat = flat.swapaxes(3, 4).reshape(2, A, B, BLOCKS * 16, LANES)
    return pl.pallas_call(
        channelize_kernel,
        name="channelize",
        in_specs=[pl.BlockSpec(memory_space=pltpu.HBM)] * 4,
        out_shape=jax.ShapeDtypeStruct((128, B, 2, 16, LANES), BF16),
        scratch_shapes=[
            pltpu.VMEM((B, 2, A, BLOCKS * 16, LANES), BF16),
            pltpu.VMEM((TAPS, NCHAN), F32),
            pltpu.VMEM((512, 512), BF16),
            pltpu.VMEM((8, 256), F32),
            pltpu.VMEM((TAPS * 16, LANES), F32),
            pltpu.VMEM((2, 2, FRAMES * 16, LANES), F32),
            pltpu.VMEM((256, 512), BF16),
            pltpu.VMEM((512 * A, LANES), F32),
            pltpu.SemaphoreType.DMA((B + 3,)),
        ],
        compiler_params=pltpu.CompilerParams(vmem_limit_bytes=40 << 20),
    )(in_hbm(flat), in_hbm(fir), in_hbm(jnp.asarray(dft_table())), in_hbm(jnp.asarray(twiddle_table())))


def beam_kernel(in_ref, row_ref, col_ref, sum_ref, out_ref, turn):
    def row_step(high, carry):
        for low in range(8):
            piece = jnp.concatenate(
                [in_ref[:, 2 * high + low // B, low % B, h].reshape(128, LANES) for h in range(2)], axis=1
            )
            got = jnp.dot(row_ref[...], piece, preferred_element_type=F32)
            for h in range(2):
                turn[h, pl.ds(high * 1024 + low, 128, stride=8), :] = got[:, h * LANES:(h + 1) * LANES]
        return carry

    lax.fori_loop(0, NCOL // 8, row_step, 0)

    def col_step(g, carry):
        pows = []
        for j in range(4):
            base = (4 * g + j) * 16
            mids = []
            for h in range(2):
                rows = [turn[h, pl.ds(pl.multiple_of(high * 1024 + base, 16), 16), :] for high in range(8)]
                mids.append(jnp.concatenate(rows, axis=0).astype(BF16))
            beam = jnp.dot(col_ref[...], jnp.concatenate(mids, axis=1), preferred_element_type=F32)
            re = beam[:NCOL]
            im = beam[NCOL:]
            pows.append((re * re + im * im).astype(BF16))
        power = jnp.concatenate(pows, axis=0)
        out_ref[g] = lax.dot_general(
            sum_ref[...], power, (((1,), (1,)), ((), ())), preferred_element_type=F32
        )
        return carry

    lax.fori_loop(0, COLS, col_step, 0)


def beamform(got):
    return pl.pallas_call(
        beam_kernel,
        name="beamform",
        out_shape=jax.ShapeDtypeStruct((COLS, 16, 256), F32),
        scratch_shapes=[pltpu.VMEM((2, 128 * NCOL, LANES), F32)],
        compiler_params=pltpu.CompilerParams(vmem_limit_bytes=40 << 20),
    )(
        got.reshape(ROWS, COLS, B, 2, 16, LANES),
        jnp.asarray(row_matrix()),
        jnp.asarray(col_matrix()),
        jnp.asarray(sum_matrix()),
    )


def finish_kernel(in_ref, out_ref):
    for p in range(POL):
        piece = in_ref[:, p * 8:(p + 1) * 8, :].reshape(128, 256)
        out_ref[pl.ds(p, 256, stride=2), :] = piece.T


def finish(got):
    return pl.pallas_call(
        finish_kernel,
        name="finish",
        out_shape=jax.ShapeDtypeStruct((256 * POL, LANES), F32),
    )(got)


def body(volts, fir):
    spectra = channelize(volts, fir)
    gathered = lax.all_to_all(spectra, ("row", "col"), 0, 0, tiled=True)
    partial = beamform(gathered)
    swapped = lax.all_to_all(partial, "col", 0, 0, tiled=True)
    return finish(swapped).reshape(NROW // COLS, NCOL, POL, LANES)


def solution(mesh):
    in_specs = (P(None, "row", "col", None, None), P())
    out_specs = P("col", None, None, "row")
    return jax.shard_map(body, mesh=mesh, in_specs=in_specs, out_specs=out_specs, check_vma=False)
```

```python
import functools

import jax
import jax.numpy as jnp
import numpy as np
from jax import lax
from jax.experimental import pallas as pl
from jax.experimental.pallas import tpu as pltpu
from jax.sharding import PartitionSpec as P

NROW = 64
NCOL = 64
POL = 2
NCHAN = 1024
TAPS = 16
FRAMES = 16
ROWS = 8
COLS = 16
A = NROW // ROWS
B = NCOL // COLS
BLOCKS = FRAMES + TAPS - 1
LANES = 128
GROUP = 16
F32 = jnp.float32
BF16 = jnp.bfloat16


def bf16_pair(angle):
    cosine = np.cos(angle).astype(np.float32).astype(jnp.bfloat16)
    sine = np.sin(angle).astype(np.float32).astype(jnp.bfloat16)
    return cosine, sine


def complex_table(angle):
    cosine, sine = bf16_pair(angle)
    real = np.stack([cosine, sine], axis=-1)
    imag = np.stack([-sine, cosine], axis=-1)
    return np.stack([real, imag], axis=1)


def dft_table():
    k = np.arange(256)
    table = complex_table(2.0 * np.pi * (np.outer(k, k) % 256) / 256)
    return table.transpose(0, 1, 3, 2).reshape(512, 512)


def twiddle_table():
    n = np.arange(256)
    angle = 2.0 * np.pi * np.outer(np.arange(4), n) / NCHAN
    return np.concatenate([np.cos(angle), np.sin(angle)]).astype(np.float32)


def spatial(length):
    index = np.arange(length)
    return complex_table(2.0 * np.pi * (np.outer(index, index) % length) / length)


def row_matrix():
    table = spatial(NROW).reshape(NROW, 2, ROWS, A, 2)
    return table.transpose(0, 1, 2, 4, 3).reshape(2 * NROW, 2 * NROW)


def col_matrix():
    table = spatial(NCOL).reshape(NCOL, 2, 8, 8, 2)
    return table.transpose(1, 0, 2, 4, 3).reshape(2 * NCOL, 2 * NCOL)


def sum_matrix():
    eye = np.eye(8, dtype=np.float32).reshape(2, 4, 2, 4)
    full = np.einsum("hqHQ,pP,f->phqHQPf", eye, np.eye(2, dtype=np.float32), np.ones(FRAMES, np.float32))
    return (full.reshape(16, 256) / (FRAMES * NROW * NCOL)).astype(jnp.bfloat16)


def channelize_kernel(x_hbm, fir_hbm, dft_hbm, tw_hbm, out_ref, x_ref, fir_ref, dft_ref, tw_ref, coef, filt, zed, turn, sems):
    x_copies = [pltpu.make_async_copy(x_hbm.at[:, :, b], x_ref.at[b], sems.at[b]) for b in range(B)]
    fir_copy = pltpu.make_async_copy(fir_hbm, fir_ref, sems.at[B])
    dft_copy = pltpu.make_async_copy(dft_hbm, dft_ref, sems.at[B + 1])
    tw_copy = pltpu.make_async_copy(tw_hbm, tw_ref, sems.at[B + 2])
    fir_copy.start()
    x_copies[0].start()
    tw_copy.start()
    dft_copy.start()
    for b in range(1, B):
        x_copies[b].start()
    fir_copy.wait()
    for s in range(8):
        piece = fir_ref[:, s * LANES:(s + 1) * LANES]
        for p in range(POL):
            coef[pl.ds(2 * s + p, TAPS, stride=16), :] = piece

    def filter_pair(index, units=((0, 0), (0, 1), (1, 0), (1, 1))):
        col = index // (A // 2)
        pair = index % (A // 2)
        for which, part in units:
                taps = [coef[16 * t:16 * t + 16, :].astype(BF16) for t in range(TAPS)]
                xs = [x_ref[col, part, 2 * pair + which, 16 * i:16 * i + 16, :] for i in range(BLOCKS)]
                for f in range(FRAMES):
                    terms = [taps[t] * xs[f + t] for t in range(TAPS)]
                    while len(terms) > TAPS // GROUP:
                        terms = [a + b for a, b in zip(terms[::2], terms[1::2])]
                    terms = [t.astype(F32) for t in terms]
                    while len(terms) > 1:
                        terms = [a + b for a, b in zip(terms[::2], terms[1::2])]
                    row = (f // 8) * 128 + f % 8
                    filt[which, part, pl.ds(row, 16, stride=8), :] = terms[0]

    def load_rows(which, part, row):
        lo = filt[which, part, row * 8:row * 8 + 8, :]
        hi = filt[which, part, 128 + row * 8:128 + row * 8 + 8, :]
        return jnp.concatenate([lo, hi], axis=0)

    def butterfly(slot):
        for which in range(2):
            for p in range(POL):
                for lo in range(2):
                    rows = [2 * (2 * j + lo) + p for j in range(4)]
                    re = [load_rows(which, 0, row) for row in rows]
                    im = [load_rows(which, 1, row) for row in rows]
                    sr0, si0 = re[0] + re[2], im[0] + im[2]
                    sr1, si1 = re[1] + re[3], im[1] + im[3]
                    dr0, di0 = re[0] - re[2], im[0] - im[2]
                    dr1, di1 = re[1] - re[3], im[1] - im[3]
                    outs = [
                        (sr0 + sr1, si0 + si1),
                        (dr0 + di1, di0 - dr1),
                        (sr0 - sr1, si0 - si1),
                        (dr0 - di1, di0 + dr1),
                    ]
                    for q in range(4):
                        zr, zi = outs[q]
                        if q > 0:
                            cosine = tw_ref[q:q + 1, lo * LANES:(lo + 1) * LANES]
                            sine = tw_ref[4 + q:5 + q, lo * LANES:(lo + 1) * LANES]
                            zr, zi = zr * cosine + zi * sine, zi * cosine - zr * sine
                        r0 = which * LANES + q * 32 + p * 16
                        zed[slot, r0:r0 + 16, lo * LANES:(lo + 1) * LANES] = zr.astype(BF16)
                        zed[slot, r0:r0 + 16, (2 + lo) * LANES:(3 + lo) * LANES] = zi.astype(BF16)

    x_copies[0].wait()
    filter_pair(0)
    tw_copy.wait()
    dft_copy.wait()

    def col_step(col, carry):
        @pl.when(col < B - 1)
        def _():
            pltpu.make_async_copy(x_hbm.at[:, :, col + 1], x_ref.at[col + 1], sems.at[col + 1]).wait()

        def pair_step(pair, carry):
            index = col * (A // 2) + pair
            butterfly(index)
            filter_pair(jnp.minimum(index + 1, B * A // 2 - 1))
            return carry

        return lax.fori_loop(0, A // 2, pair_step, carry)

    lax.fori_loop(0, B, col_step, 0)

    def transform_step(col, carry):
        for pair in range(A // 2):
            spec = lax.dot_general(
                dft_ref[...], zed[col * (A // 2) + pair], (((1,), (1,)), ((), ())), preferred_element_type=F32
            )
            for which in range(2):
                turn[pl.ds(2 * pair + which, 512, stride=A), :] = spec[:, which * LANES:(which + 1) * LANES]
        out_ref[:, col] = turn[...].reshape(128, 2, 16, LANES).astype(BF16)
        return carry

    lax.fori_loop(0, B, transform_step, 0)


def in_hbm(x):
    return pltpu.with_memory_space_constraint(x, pltpu.HBM)


def channelize(volts, fir):
    flat = volts.reshape(2, A, B, POL, BLOCKS * 8, LANES)
    flat = flat.swapaxes(3, 4).reshape(2, A, B, BLOCKS * 16, LANES)
    return pl.pallas_call(
        channelize_kernel,
        name="channelize",
        in_specs=[pl.BlockSpec(memory_space=pltpu.HBM)] * 4,
        out_shape=jax.ShapeDtypeStruct((128, B, 2, 16, LANES), BF16),
        scratch_shapes=[
            pltpu.VMEM((B, 2, A, BLOCKS * 16, LANES), BF16),
            pltpu.VMEM((TAPS, NCHAN), F32),
            pltpu.VMEM((512, 512), BF16),
            pltpu.VMEM((8, 256), F32),
            pltpu.VMEM((TAPS * 16, LANES), F32),
            pltpu.VMEM((2, 2, FRAMES * 16, LANES), F32),
            pltpu.VMEM((B * A // 2, 256, 512), BF16),
            pltpu.VMEM((512 * A, LANES), F32),
            pltpu.SemaphoreType.DMA((B + 3,)),
        ],
        compiler_params=pltpu.CompilerParams(vmem_limit_bytes=40 << 20),
    )(in_hbm(flat), in_hbm(fir), in_hbm(jnp.asarray(dft_table())), in_hbm(jnp.asarray(twiddle_table())))


def beam_kernel(in_ref, row_ref, col_ref, sum_ref, out_ref, turn):
    def row_step(high, carry):
        for low in range(8):
            piece = jnp.concatenate(
                [in_ref[:, 2 * high + low // B, low % B, h].reshape(128, LANES) for h in range(2)], axis=1
            )
            got = jnp.dot(row_ref[...], piece, preferred_element_type=F32)
            for h in range(2):
                turn[h, pl.ds(high * 1024 + low, 128, stride=8), :] = got[:, h * LANES:(h + 1) * LANES]
        return carry

    lax.fori_loop(0, NCOL // 8, row_step, 0, unroll=2)

    def col_step(g, carry):
        pows = []
        for j in range(4):
            base = (4 * g + j) * 16
            mids = []
            for h in range(2):
                rows = [turn[h, pl.ds(pl.multiple_of(high * 1024 + base, 16), 16), :] for high in range(8)]
                mids.append(jnp.concatenate(rows, axis=0).astype(BF16))
            beam = jnp.dot(col_ref[...], jnp.concatenate(mids, axis=1), preferred_element_type=F32)
            re = beam[:NCOL]
            im = beam[NCOL:]
            pows.append((re * re + im * im).astype(BF16))
        power = jnp.concatenate(pows, axis=0)
        out_ref[g] = lax.dot_general(
            sum_ref[...], power, (((1,), (1,)), ((), ())), preferred_element_type=F32
        )
        return carry

    lax.fori_loop(0, COLS, col_step, 0, unroll=4)


def beamform(got):
    return pl.pallas_call(
        beam_kernel,
        name="beamform",
        out_shape=jax.ShapeDtypeStruct((COLS, 16, 256), F32),
        scratch_shapes=[pltpu.VMEM((2, 128 * NCOL, LANES), F32)],
        compiler_params=pltpu.CompilerParams(vmem_limit_bytes=40 << 20),
    )(
        got.reshape(ROWS, COLS, B, 2, 16, LANES),
        jnp.asarray(row_matrix()),
        jnp.asarray(col_matrix()),
        jnp.asarray(sum_matrix()),
    )


def finish_kernel(in_ref, out_ref):
    for p in range(POL):
        piece = in_ref[:, p * 8:(p + 1) * 8, :].reshape(128, 256)
        out_ref[pl.ds(p, 256, stride=2), :] = piece.T


def finish(got):
    return pl.pallas_call(
        finish_kernel,
        name="finish",
        out_shape=jax.ShapeDtypeStruct((256 * POL, LANES), F32),
    )(got)


def body(volts, fir):
    spectra = channelize(volts, fir)
    gathered = lax.all_to_all(spectra, ("row", "col"), 0, 0, tiled=True)
    partial = beamform(gathered)
    swapped = lax.all_to_all(partial, "col", 0, 0, tiled=True)
    return finish(swapped).reshape(NROW // COLS, NCOL, POL, LANES)


def solution(mesh):
    in_specs = (P(None, "row", "col", None, None), P())
    out_specs = P("col", None, None, "row")
    return jax.shard_map(body, mesh=mesh, in_specs=in_specs, out_specs=out_specs, check_vma=False)
```

```python
import functools

import jax
import jax.numpy as jnp
import numpy as np
from jax import lax
from jax.experimental import pallas as pl
from jax.experimental.pallas import tpu as pltpu
from jax.sharding import PartitionSpec as P

NROW = 64
NCOL = 64
POL = 2
NCHAN = 1024
TAPS = 16
FRAMES = 16
ROWS = 8
COLS = 16
A = NROW // ROWS
B = NCOL // COLS
BLOCKS = FRAMES + TAPS - 1
LANES = 128
GROUP = 16
F32 = jnp.float32
BF16 = jnp.bfloat16


def bf16_pair(angle):
    cosine = np.cos(angle).astype(np.float32).astype(jnp.bfloat16)
    sine = np.sin(angle).astype(np.float32).astype(jnp.bfloat16)
    return cosine, sine


def complex_table(angle):
    cosine, sine = bf16_pair(angle)
    real = np.stack([cosine, sine], axis=-1)
    imag = np.stack([-sine, cosine], axis=-1)
    return np.stack([real, imag], axis=1)


def dft_table():
    k = np.arange(256)
    table = complex_table(2.0 * np.pi * (np.outer(k, k) % 256) / 256)
    return table.transpose(0, 1, 3, 2).reshape(512, 512)


def twiddle_table():
    n = np.arange(256)
    angle = 2.0 * np.pi * np.outer(np.arange(4), n) / NCHAN
    return np.concatenate([np.cos(angle), np.sin(angle)]).astype(np.float32)


def spatial(length):
    index = np.arange(length)
    return complex_table(2.0 * np.pi * (np.outer(index, index) % length) / length)


def row_matrix():
    table = spatial(NROW).reshape(NROW, 2, ROWS, A, 2)
    return table.transpose(0, 1, 2, 4, 3).reshape(2 * NROW, 2 * NROW)


def col_matrix():
    table = spatial(NCOL).reshape(NCOL, 2, 8, 8, 2)
    return table.transpose(1, 0, 2, 4, 3).reshape(2 * NCOL, 2 * NCOL)


def sum_matrix():
    eye = np.eye(8, dtype=np.float32).reshape(2, 4, 2, 4)
    full = np.einsum("hqHQ,pP,f->phqHQPf", eye, np.eye(2, dtype=np.float32), np.ones(FRAMES, np.float32))
    return (full.reshape(16, 256) / (FRAMES * NROW * NCOL)).astype(jnp.bfloat16)


def channelize_kernel(x_hbm, fir_hbm, dft_hbm, tw_hbm, out_ref, x_ref, fir_ref, dft_ref, tw_ref, coef, filt, zed, turn, sems):
    x_copies = [pltpu.make_async_copy(x_hbm.at[:, :, b], x_ref.at[b], sems.at[b]) for b in range(1, B)]
    head_copy = pltpu.make_async_copy(x_hbm.at[:, :2, 0], x_ref.at[0, :, :2], sems.at[0])
    tail_copy = pltpu.make_async_copy(x_hbm.at[:, 2:, 0], x_ref.at[0, :, 2:], sems.at[B + 3])
    fir_copy = pltpu.make_async_copy(fir_hbm, fir_ref, sems.at[B])
    dft_copy = pltpu.make_async_copy(dft_hbm, dft_ref, sems.at[B + 1])
    tw_copy = pltpu.make_async_copy(tw_hbm, tw_ref, sems.at[B + 2])
    fir_copy.start()
    head_copy.start()
    tail_copy.start()
    tw_copy.start()
    for copy in x_copies:
        copy.start()
    dft_copy.start()
    fir_copy.wait()
    for s in range(8):
        piece = fir_ref[:, s * LANES:(s + 1) * LANES]
        for p in range(POL):
            coef[pl.ds(2 * s + p, TAPS, stride=16), :] = piece

    def filter_pair(index, units=((0, 0), (0, 1), (1, 0), (1, 1))):
        col = index // (A // 2)
        pair = index % (A // 2)
        for which, part in units:
                taps = [coef[16 * t:16 * t + 16, :].astype(BF16) for t in range(TAPS)]
                xs = [x_ref[col, part, 2 * pair + which, 16 * i:16 * i + 16, :] for i in range(BLOCKS)]
                for f in range(FRAMES):
                    terms = [taps[t] * xs[f + t] for t in range(TAPS)]
                    while len(terms) > TAPS // GROUP:
                        terms = [a + b for a, b in zip(terms[::2], terms[1::2])]
                    terms = [t.astype(F32) for t in terms]
                    while len(terms) > 1:
                        terms = [a + b for a, b in zip(terms[::2], terms[1::2])]
                    row = (f // 8) * 128 + f % 8
                    filt[which, part, pl.ds(row, 16, stride=8), :] = terms[0]

    def load_rows(which, part, row):
        lo = filt[which, part, row * 8:row * 8 + 8, :]
        hi = filt[which, part, 128 + row * 8:128 + row * 8 + 8, :]
        return jnp.concatenate([lo, hi], axis=0)

    def butterfly(slot):
        for which in range(2):
            for p in range(POL):
                for lo in range(2):
                    rows = [2 * (2 * j + lo) + p for j in range(4)]
                    re = [load_rows(which, 0, row) for row in rows]
                    im = [load_rows(which, 1, row) for row in rows]
                    sr0, si0 = re[0] + re[2], im[0] + im[2]
                    sr1, si1 = re[1] + re[3], im[1] + im[3]
                    dr0, di0 = re[0] - re[2], im[0] - im[2]
                    dr1, di1 = re[1] - re[3], im[1] - im[3]
                    outs = [
                        (sr0 + sr1, si0 + si1),
                        (dr0 + di1, di0 - dr1),
                        (sr0 - sr1, si0 - si1),
                        (dr0 - di1, di0 + dr1),
                    ]
                    for q in range(4):
                        zr, zi = outs[q]
                        if q > 0:
                            cosine = tw_ref[q:q + 1, lo * LANES:(lo + 1) * LANES]
                            sine = tw_ref[4 + q:5 + q, lo * LANES:(lo + 1) * LANES]
                            zr, zi = zr * cosine + zi * sine, zi * cosine - zr * sine
                        r0 = which * LANES + q * 32 + p * 16
                        zed[slot, r0:r0 + 16, lo * LANES:(lo + 1) * LANES] = zr.astype(BF16)
                        zed[slot, r0:r0 + 16, (2 + lo) * LANES:(3 + lo) * LANES] = zi.astype(BF16)

    head_copy.wait()
    filter_pair(0)
    tw_copy.wait()
    tail_copy.wait()

    def pair_step(index, carry):
        col = (index + 1) // (A // 2)

        @pl.when(index % (A // 2) == A // 2 - 1)
        def _():
            pltpu.make_async_copy(x_hbm.at[:, :, col], x_ref.at[col], sems.at[col]).wait()

        butterfly(index)
        filter_pair(index + 1)
        return carry

    lax.fori_loop(0, B * A // 2 - 1, pair_step, 0)
    butterfly(B * A // 2 - 1)
    dft_copy.wait()

    def transform_step(col, carry):
        for pair in range(A // 2):
            spec = lax.dot_general(
                dft_ref[...], zed[col * (A // 2) + pair], (((1,), (1,)), ((), ())), preferred_element_type=F32
            )
            for which in range(2):
                turn[pl.ds(2 * pair + which, 512, stride=A), :] = spec[:, which * LANES:(which + 1) * LANES]
        out_ref[:, col] = turn[...].reshape(128, 2, 16, LANES).astype(BF16)
        return carry

    lax.fori_loop(0, B, transform_step, 0)


def in_hbm(x):
    return pltpu.with_memory_space_constraint(x, pltpu.HBM)


def channelize(volts, fir):
    flat = volts.reshape(2, A, B, POL, BLOCKS * 8, LANES)
    flat = flat.swapaxes(3, 4).reshape(2, A, B, BLOCKS * 16, LANES)
    return pl.pallas_call(
        channelize_kernel,
        name="channelize",
        in_specs=[pl.BlockSpec(memory_space=pltpu.HBM)] * 4,
        out_shape=jax.ShapeDtypeStruct((128, B, 2, 16, LANES), BF16),
        scratch_shapes=[
            pltpu.VMEM((B, 2, A, BLOCKS * 16, LANES), BF16),
            pltpu.VMEM((TAPS, NCHAN), F32),
            pltpu.VMEM((512, 512), BF16),
            pltpu.VMEM((8, 256), F32),
            pltpu.VMEM((TAPS * 16, LANES), F32),
            pltpu.VMEM((2, 2, FRAMES * 16, LANES), F32),
            pltpu.VMEM((B * A // 2, 256, 512), BF16),
            pltpu.VMEM((512 * A, LANES), F32),
            pltpu.SemaphoreType.DMA((B + 4,)),
        ],
        compiler_params=pltpu.CompilerParams(vmem_limit_bytes=40 << 20),
    )(in_hbm(flat), in_hbm(fir), in_hbm(jnp.asarray(dft_table())), in_hbm(jnp.asarray(twiddle_table())))


def beam_kernel(in_ref, row_ref, col_ref, sum_ref, out_ref, turn):
    def row_step(high, carry):
        for low in range(8):
            piece = jnp.concatenate(
                [in_ref[:, 2 * high + low // B, low % B, h].reshape(128, LANES) for h in range(2)], axis=1
            )
            got = jnp.dot(row_ref[...], piece, preferred_element_type=F32)
            for h in range(2):
                turn[h, pl.ds(high * 1024 + low, 128, stride=8), :] = got[:, h * LANES:(h + 1) * LANES]
        return carry

    lax.fori_loop(0, NCOL // 8, row_step, 0, unroll=8)

    def col_step(g, carry):
        pows = []
        for j in range(4):
            base = (4 * g + j) * 16
            mids = []
            for h in range(2):
                rows = [turn[h, pl.ds(pl.multiple_of(high * 1024 + base, 16), 16), :] for high in range(8)]
                mids.append(jnp.concatenate(rows, axis=0).astype(BF16))
            beam = jnp.dot(col_ref[...], jnp.concatenate(mids, axis=1), preferred_element_type=F32)
            re = beam[:NCOL]
            im = beam[NCOL:]
            pows.append((re * re + im * im).astype(BF16))
        power = jnp.concatenate(pows, axis=0)
        out_ref[g] = lax.dot_general(
            sum_ref[...], power, (((1,), (1,)), ((), ())), preferred_element_type=F32
        )
        return carry

    lax.fori_loop(0, COLS, col_step, 0, unroll=16)


def beamform(got):
    return pl.pallas_call(
        beam_kernel,
        name="beamform",
        out_shape=jax.ShapeDtypeStruct((COLS, 16, 256), F32),
        scratch_shapes=[pltpu.VMEM((2, 128 * NCOL, LANES), F32)],
        compiler_params=pltpu.CompilerParams(vmem_limit_bytes=40 << 20),
    )(
        got.reshape(ROWS, COLS, B, 2, 16, LANES),
        jnp.asarray(row_matrix()),
        jnp.asarray(col_matrix()),
        jnp.asarray(sum_matrix()),
    )


def finish_kernel(in_ref, out_ref):
    for p in range(POL):
        piece = in_ref[:, p * 8:(p + 1) * 8, :].reshape(128, 256)
        out_ref[pl.ds(p, 256, stride=2), :] = piece.T


def finish(got):
    return pl.pallas_call(
        finish_kernel,
        name="finish",
        in_specs=[pl.BlockSpec(memory_space=pltpu.VMEM)],
        out_shape=jax.ShapeDtypeStruct((256 * POL, LANES), F32),
    )(pltpu.with_memory_space_constraint(got, pltpu.VMEM))


def body(volts, fir):
    spectra = channelize(volts, fir)
    gathered = lax.all_to_all(spectra, ("row", "col"), 0, 0, tiled=True)
    partial = beamform(gathered)
    swapped = lax.all_to_all(partial, "col", 0, 0, tiled=True)
    return finish(swapped).reshape(NROW // COLS, NCOL, POL, LANES)


def solution(mesh):
    in_specs = (P(None, "row", "col", None, None), P())
    out_specs = P("col", None, None, "row")
    return jax.shard_map(body, mesh=mesh, in_specs=in_specs, out_specs=out_specs, check_vma=False)
```

```python
import functools

import math

import jax
import jax.numpy as jnp
import numpy as np
from jax import lax
from jax.experimental import pallas as pl
from jax.experimental.pallas import tpu as pltpu
from jax.sharding import PartitionSpec as P

NROW = 64
NCOL = 64
POL = 2
NCHAN = 1024
TAPS = 16
FRAMES = 16
ROWS = 8
COLS = 16
A = NROW // ROWS
B = NCOL // COLS
BLOCKS = FRAMES + TAPS - 1
LANES = 128
GROUP = 16
F32 = jnp.float32
BF16 = jnp.bfloat16


def bf16_pair(angle):
    cosine = np.cos(angle).astype(np.float32).astype(jnp.bfloat16)
    sine = np.sin(angle).astype(np.float32).astype(jnp.bfloat16)
    return cosine, sine


def complex_table(angle):
    cosine, sine = bf16_pair(angle)
    real = np.stack([cosine, sine], axis=-1)
    imag = np.stack([-sine, cosine], axis=-1)
    return np.stack([real, imag], axis=1)


def dft_table():
    k = np.arange(LANES)
    table = complex_table(2.0 * np.pi * (np.outer(k, k) % LANES) / LANES)
    return table.transpose(0, 1, 3, 2).reshape(2 * LANES, 2 * LANES)


def twiddle_table():
    angle = 2.0 * np.pi * np.outer(np.arange(8), np.arange(LANES)) / NCHAN
    return np.concatenate([np.cos(angle), np.sin(angle)]).astype(np.float32)


def spatial(length):
    index = np.arange(length)
    return complex_table(2.0 * np.pi * (np.outer(index, index) % length) / length)


def row_matrix():
    table = spatial(NROW).reshape(NROW, 2, ROWS, A // 4, 4, 2)
    return table.transpose(0, 1, 2, 3, 5, 4).reshape(2 * NROW, 2 * NROW)


def col_matrix():
    table = spatial(NCOL).reshape(NCOL, 2, COLS, B, 2)
    return table.transpose(1, 0, 2, 4, 3).reshape(2 * NCOL, 2 * NCOL)


def sum_matrix():
    eye = np.eye(8, dtype=np.float32).reshape(2, 4, 2, 4)
    ones = np.ones(4, np.float32)
    full = np.einsum("hqHQ,pP,g,f->phqHQgPf", eye, np.eye(2, dtype=np.float32), ones, ones)
    return (full.reshape(16, 256) / (FRAMES * NROW * NCOL)).astype(jnp.bfloat16)


def channelize_kernel(x_hbm, fir_hbm, dft_hbm, tw_hbm, out_ref, x_ref, fir_ref, dft_ref, tw_ref, coef, filt, zed, turn, sems):
    x_copies = [pltpu.make_async_copy(x_hbm.at[:, :, b], x_ref.at[b], sems.at[b]) for b in range(1, B)]
    head_copy = pltpu.make_async_copy(x_hbm.at[:, :2, 0], x_ref.at[0, :, :2], sems.at[0])
    tail_copy = pltpu.make_async_copy(x_hbm.at[:, 2:, 0], x_ref.at[0, :, 2:], sems.at[B + 3])
    fir_copy = pltpu.make_async_copy(fir_hbm, fir_ref, sems.at[B])
    dft_copy = pltpu.make_async_copy(dft_hbm, dft_ref, sems.at[B + 1])
    tw_copy = pltpu.make_async_copy(tw_hbm, tw_ref, sems.at[B + 2])
    fir_copy.start()
    head_copy.start()
    tail_copy.start()
    tw_copy.start()
    for copy in x_copies:
        copy.start()
    dft_copy.start()
    fir_copy.wait()
    for s in range(8):
        piece = fir_ref[:, s * LANES:(s + 1) * LANES]
        for p in range(POL):
            coef[pl.ds(2 * s + p, TAPS, stride=16), :] = piece

    def filter_pair(index, units=((0, 0), (0, 1), (1, 0), (1, 1))):
        col = index // (A // 2)
        pair = index % (A // 2)
        for which, part in units:
                taps = [coef[16 * t:16 * t + 16, :].astype(BF16) for t in range(TAPS)]
                xs = [x_ref[col, part, 2 * pair + which, 16 * i:16 * i + 16, :] for i in range(BLOCKS)]
                for f in range(FRAMES):
                    terms = [taps[t] * xs[f + t] for t in range(TAPS)]
                    while len(terms) > TAPS // GROUP:
                        terms = [a + b for a, b in zip(terms[::2], terms[1::2])]
                    terms = [t.astype(F32) for t in terms]
                    while len(terms) > 1:
                        terms = [a + b for a, b in zip(terms[::2], terms[1::2])]
                    row = (f // 4) * 64 + f % 4
                    filt[which, part, pl.ds(row, 16, stride=4), :] = terms[0]

    def load_rows(which, part, t, j):
        lo = filt[which, part, 128 * t + 8 * j:128 * t + 8 * j + 8, :]
        hi = filt[which, part, 128 * t + 64 + 8 * j:128 * t + 64 + 8 * j + 8, :]
        return jnp.concatenate([lo, hi], axis=0)

    def dft4(y):
        (r0, i0), (r1, i1), (r2, i2), (r3, i3) = y
        sr0, si0 = r0 + r2, i0 + i2
        sr1, si1 = r1 + r3, i1 + i3
        dr0, di0 = r0 - r2, i0 - i2
        dr1, di1 = r1 - r3, i1 - i3
        return [
            (sr0 + sr1, si0 + si1),
            (dr0 + di1, di0 - dr1),
            (sr0 - sr1, si0 - si1),
            (dr0 - di1, di0 + dr1),
        ]

    def butterfly(slot):
        half = math.sqrt(0.5)
        for which in range(2):
            for t in range(2):
                re = [load_rows(which, 0, t, j) for j in range(8)]
                im = [load_rows(which, 1, t, j) for j in range(8)]
                sums = [(re[j] + re[j + 4], im[j] + im[j + 4]) for j in range(4)]
                (r0, i0), (r1, i1), (r2, i2), (r3, i3) = [
                    (re[j] - re[j + 4], im[j] - im[j + 4]) for j in range(4)
                ]
                odds = [
                    (r0, i0),
                    ((r1 + i1) * half, (i1 - r1) * half),
                    (i2, -r2),
                    ((i3 - r3) * half, (r3 + i3) * -half),
                ]
                for parity, outs in enumerate((dft4(sums), dft4(odds))):
                    for r in range(4):
                        q = 2 * r + parity
                        zr, zi = outs[r]
                        if q > 0:
                            cosine = tw_ref[q:q + 1, :]
                            sine = tw_ref[8 + q:9 + q, :]
                            zr, zi = zr * cosine + zi * sine, zi * cosine - zr * sine
                        row = q * 32 + t * 16
                        zed[2 * slot + which, row:row + 16, :LANES] = zr.astype(BF16)
                        zed[2 * slot + which, row:row + 16, LANES:] = zi.astype(BF16)

    head_copy.wait()
    filter_pair(0)
    tw_copy.wait()
    tail_copy.wait()

    def pair_step(index, carry):
        col = (index + 1) // (A // 2)

        @pl.when(index % (A // 2) == A // 2 - 1)
        def _():
            pltpu.make_async_copy(x_hbm.at[:, :, col], x_ref.at[col], sems.at[col]).wait()

        butterfly(index)
        filter_pair(index + 1)
        return carry

    lax.fori_loop(0, B * A // 2 - 1, pair_step, 0)
    butterfly(B * A // 2 - 1)
    dft_copy.wait()

    def transform_step(col, carry):
        for ant in range(A):
            spec = lax.dot_general(
                dft_ref[...], zed[col * A + ant], (((1,), (1,)), ((), ())), preferred_element_type=F32
            )
            for h in range(2):
                row = (2 * h + ant // 4) * 1024 + ant % 4
                turn[col % 2, pl.ds(row, 256, stride=4), :] = spec[:, h * LANES:(h + 1) * LANES]
        for h in range(2):
            rows = [turn[col % 2, i * 1024:(i + 1) * 1024, :].reshape(128, 8, LANES) for i in (2 * h, 2 * h + 1)]
            out_ref[:, col, h] = jnp.concatenate(rows, axis=1).astype(BF16)
        return carry

    for col in range(B):
        transform_step(col, 0)


def in_hbm(x):
    return pltpu.with_memory_space_constraint(x, pltpu.HBM)


def channelize(volts, fir):
    flat = volts.reshape(2, A, B, POL, BLOCKS * 8, LANES)
    flat = flat.swapaxes(3, 4).reshape(2, A, B, BLOCKS * 16, LANES)
    return pl.pallas_call(
        channelize_kernel,
        name="channelize",
        in_specs=[pl.BlockSpec(memory_space=pltpu.HBM)] * 4,
        out_shape=jax.ShapeDtypeStruct((128, B, 2, 16, LANES), BF16),
        scratch_shapes=[
            pltpu.VMEM((B, 2, A, BLOCKS * 16, LANES), BF16),
            pltpu.VMEM((TAPS, NCHAN), F32),
            pltpu.VMEM((256, 256), BF16),
            pltpu.VMEM((16, LANES), F32),
            pltpu.VMEM((TAPS * 16, LANES), F32),
            pltpu.VMEM((2, 2, FRAMES * 16, LANES), F32),
            pltpu.VMEM((B * A, 256, 256), BF16),
            pltpu.VMEM((2, 512 * A, LANES), F32),
            pltpu.SemaphoreType.DMA((B + 4,)),
        ],
        compiler_params=pltpu.CompilerParams(vmem_limit_bytes=40 << 20),
    )(in_hbm(flat), in_hbm(fir), in_hbm(jnp.asarray(dft_table())), in_hbm(jnp.asarray(twiddle_table())))


def beam_kernel(in_ref, row_ref, col_ref, sum_ref, out_ref, turn):
    def row_step(high, carry):
        for low in range(8):
            piece = jnp.concatenate(
                [in_ref[:, 2 * high + low // B, low % B, h].reshape(128, LANES) for h in range(2)], axis=1
            )
            got = jnp.dot(row_ref[...], piece, preferred_element_type=F32)
            for h in range(2):
                turn[h, pl.ds((2 * high + low // B) * 512 + low % B, 128, stride=4), :] = got[:, h * LANES:(h + 1) * LANES]
        return carry

    lax.fori_loop(0, NCOL // 8, row_step, 0, unroll=8)

    def col_step(g, carry):
        pows = []
        for j in range(4):
            base = (4 * g + j) * 8
            mids = []
            for h in range(2):
                rows = [turn[h, pl.ds(pl.multiple_of(c * 512 + base, 8), 8), :] for c in range(COLS)]
                mids.append(jnp.concatenate(rows, axis=0).astype(BF16))
            beam = jnp.dot(col_ref[...], jnp.concatenate(mids, axis=1), preferred_element_type=F32)
            re = beam[:NCOL]
            im = beam[NCOL:]
            pows.append((re * re + im * im).astype(BF16))
        power = jnp.concatenate(pows, axis=0)
        out_ref[g] = lax.dot_general(
            sum_ref[...], power, (((1,), (1,)), ((), ())), preferred_element_type=F32
        )
        return carry

    lax.fori_loop(0, COLS, col_step, 0, unroll=16)


def beamform(got):
    return pl.pallas_call(
        beam_kernel,
        name="beamform",
        out_shape=jax.ShapeDtypeStruct((COLS, 16, 256), F32),
        scratch_shapes=[pltpu.VMEM((2, 128 * NCOL, LANES), F32)],
        compiler_params=pltpu.CompilerParams(vmem_limit_bytes=40 << 20),
    )(
        got.reshape(ROWS, COLS, B, 2, 16, LANES),
        jnp.asarray(row_matrix()),
        jnp.asarray(col_matrix()),
        jnp.asarray(sum_matrix()),
    )


def finish_kernel(in_ref, out_ref):
    for p in range(POL):
        piece = in_ref[:, p * 8:(p + 1) * 8, :].reshape(128, 256)
        out_ref[pl.ds(p, 256, stride=2), :] = piece.T


def finish(got):
    return pl.pallas_call(
        finish_kernel,
        name="finish",
        in_specs=[pl.BlockSpec(memory_space=pltpu.VMEM)],
        out_shape=jax.ShapeDtypeStruct((256 * POL, LANES), F32),
    )(pltpu.with_memory_space_constraint(got, pltpu.VMEM))


def body(volts, fir):
    spectra = channelize(volts, fir)
    gathered = lax.all_to_all(spectra, ("row", "col"), 0, 0, tiled=True)
    partial = beamform(gathered)
    swapped = lax.all_to_all(partial, "col", 0, 0, tiled=True)
    return finish(swapped).reshape(NROW // COLS, NCOL, POL, LANES)


def solution(mesh):
    in_specs = (P(None, "row", "col", None, None), P())
    out_specs = P("col", None, None, "row")
    return jax.shard_map(body, mesh=mesh, in_specs=in_specs, out_specs=out_specs, check_vma=False)
```

```python
import functools

import math

import jax
import jax.numpy as jnp
import numpy as np
from jax import lax
from jax.experimental import pallas as pl
from jax.experimental.pallas import tpu as pltpu
from jax.sharding import PartitionSpec as P

NROW = 64
NCOL = 64
POL = 2
NCHAN = 1024
TAPS = 16
FRAMES = 16
ROWS = 8
COLS = 16
A = NROW // ROWS
B = NCOL // COLS
BLOCKS = FRAMES + TAPS - 1
LANES = 128
GROUP = 16
F32 = jnp.float32
BF16 = jnp.bfloat16


def bf16_pair(angle):
    cosine = np.cos(angle).astype(np.float32).astype(jnp.bfloat16)
    sine = np.sin(angle).astype(np.float32).astype(jnp.bfloat16)
    return cosine, sine


def complex_table(angle):
    cosine, sine = bf16_pair(angle)
    real = np.stack([cosine, sine], axis=-1)
    imag = np.stack([-sine, cosine], axis=-1)
    return np.stack([real, imag], axis=1)


def dft_table():
    k = np.arange(LANES)
    table = complex_table(2.0 * np.pi * (np.outer(k, k) % LANES) / LANES)
    return table.transpose(0, 1, 3, 2).reshape(2 * LANES, 2 * LANES)


def twiddle_table():
    angle = 2.0 * np.pi * np.outer(np.arange(8), np.arange(LANES)) / NCHAN
    return np.concatenate([np.cos(angle), np.sin(angle)]).astype(np.float32)


def spatial(length):
    index = np.arange(length)
    return complex_table(2.0 * np.pi * (np.outer(index, index) % length) / length)


def row_matrix():
    table = spatial(NROW).reshape(NROW, 2, ROWS, A // 4, 4, 2)
    return table.transpose(0, 1, 2, 3, 5, 4).reshape(2 * NROW, 2 * NROW)


def col_matrix():
    table = spatial(NCOL).reshape(NCOL, 2, COLS, B, 2)
    return table.transpose(1, 0, 2, 4, 3).reshape(2 * NCOL, 2 * NCOL)


def sum_matrix():
    eye = np.eye(8, dtype=np.float32).reshape(2, 4, 2, 4)
    ones = np.ones(4, np.float32)
    full = np.einsum("hqHQ,pP,g,f->phqHQgPf", eye, np.eye(2, dtype=np.float32), ones, ones)
    return (full.reshape(16, 256) / (FRAMES * NROW * NCOL)).astype(jnp.bfloat16)


def channelize_kernel(x_hbm, fir_hbm, dft_hbm, tw_hbm, out_ref, x_ref, fir_ref, dft_ref, tw_ref, coef, coef16, filt, zed, turn, sems):
    x_copies = [pltpu.make_async_copy(x_hbm.at[:, :, b], x_ref.at[b], sems.at[b]) for b in range(1, B)]
    head_copy = pltpu.make_async_copy(x_hbm.at[:, :2, 0], x_ref.at[0, :, :2], sems.at[0])
    tail_copy = pltpu.make_async_copy(x_hbm.at[:, 2:, 0], x_ref.at[0, :, 2:], sems.at[B + 3])
    fir_copy = pltpu.make_async_copy(fir_hbm, fir_ref, sems.at[B])
    dft_copy = pltpu.make_async_copy(dft_hbm, dft_ref, sems.at[B + 1])
    tw_copy = pltpu.make_async_copy(tw_hbm, tw_ref, sems.at[B + 2])
    fir_copy.start()
    head_copy.start()
    tail_copy.start()
    tw_copy.start()
    for copy in x_copies:
        copy.start()
    dft_copy.start()
    fir_copy.wait()
    for s in range(8):
        piece = fir_ref[:, s * LANES:(s + 1) * LANES]
        for p in range(POL):
            coef[pl.ds(2 * s + p, TAPS, stride=16), :] = piece
    coef16[...] = coef[...].astype(BF16)

    def filter_pair(index, units=((0, 0), (0, 1), (1, 0), (1, 1))):
        col = index // (A // 2)
        pair = index % (A // 2)
        for which, part in units:
                taps = [coef16[16 * t:16 * t + 16, :] for t in range(TAPS)]
                xs = [x_ref[col, part, 2 * pair + which, 16 * i:16 * i + 16, :] for i in range(BLOCKS)]
                for f in range(FRAMES):
                    terms = [taps[t] * xs[f + t] for t in range(TAPS)]
                    while len(terms) > TAPS // GROUP:
                        terms = [a + b for a, b in zip(terms[::2], terms[1::2])]
                    terms = [t.astype(F32) for t in terms]
                    while len(terms) > 1:
                        terms = [a + b for a, b in zip(terms[::2], terms[1::2])]
                    row = (f // 4) * 64 + f % 4
                    filt[which, part, pl.ds(row, 16, stride=4), :] = terms[0]

    def load_rows(which, part, t, j):
        lo = filt[which, part, 128 * t + 8 * j:128 * t + 8 * j + 8, :]
        hi = filt[which, part, 128 * t + 64 + 8 * j:128 * t + 64 + 8 * j + 8, :]
        return jnp.concatenate([lo, hi], axis=0)

    def dft4(y):
        (r0, i0), (r1, i1), (r2, i2), (r3, i3) = y
        sr0, si0 = r0 + r2, i0 + i2
        sr1, si1 = r1 + r3, i1 + i3
        dr0, di0 = r0 - r2, i0 - i2
        dr1, di1 = r1 - r3, i1 - i3
        return [
            (sr0 + sr1, si0 + si1),
            (dr0 + di1, di0 - dr1),
            (sr0 - sr1, si0 - si1),
            (dr0 - di1, di0 + dr1),
        ]

    def butterfly(slot):
        half = math.sqrt(0.5)
        for which in range(2):
            for t in range(2):
                re = [load_rows(which, 0, t, j) for j in range(8)]
                im = [load_rows(which, 1, t, j) for j in range(8)]
                sums = [(re[j] + re[j + 4], im[j] + im[j + 4]) for j in range(4)]
                (r0, i0), (r1, i1), (r2, i2), (r3, i3) = [
                    (re[j] - re[j + 4], im[j] - im[j + 4]) for j in range(4)
                ]
                odds = [
                    (r0, i0),
                    ((r1 + i1) * half, (i1 - r1) * half),
                    (i2, -r2),
                    ((i3 - r3) * half, (r3 + i3) * -half),
                ]
                for parity, outs in enumerate((dft4(sums), dft4(odds))):
                    for r in range(4):
                        q = 2 * r + parity
                        zr, zi = outs[r]
                        if q > 0:
                            cosine = tw_ref[q:q + 1, :]
                            sine = tw_ref[8 + q:9 + q, :]
                            zr, zi = zr * cosine + zi * sine, zi * cosine - zr * sine
                        row = q * 32 + t * 16
                        zed[2 * slot + which, row:row + 16, :LANES] = zr.astype(BF16)
                        zed[2 * slot + which, row:row + 16, LANES:] = zi.astype(BF16)

    head_copy.wait()
    filter_pair(0)
    tw_copy.wait()
    tail_copy.wait()

    def pair_step(index, carry):
        col = (index + 1) // (A // 2)

        @pl.when(index % (A // 2) == A // 2 - 1)
        def _():
            pltpu.make_async_copy(x_hbm.at[:, :, col], x_ref.at[col], sems.at[col]).wait()

        butterfly(index)
        filter_pair(index + 1)
        return carry

    lax.fori_loop(0, B * A // 2 - 1, pair_step, 0)
    butterfly(B * A // 2 - 1)
    dft_copy.wait()

    def transform_step(col, carry):
        for ant in range(A):
            spec = lax.dot_general(
                dft_ref[...], zed[col * A + ant], (((1,), (1,)), ((), ())), preferred_element_type=F32
            )
            for h in range(2):
                row = (2 * h + ant // 4) * 1024 + ant % 4
                turn[col % 2, pl.ds(row, 256, stride=4), :] = spec[:, h * LANES:(h + 1) * LANES]
        for h in range(2):
            rows = [turn[col % 2, i * 1024:(i + 1) * 1024, :].reshape(128, 8, LANES) for i in (2 * h, 2 * h + 1)]
            out_ref[:, col, h] = jnp.concatenate(rows, axis=1).astype(BF16)
        return carry

    for col in range(B):
        transform_step(col, 0)


def in_hbm(x):
    return pltpu.with_memory_space_constraint(x, pltpu.HBM)


def channelize(volts, fir):
    flat = volts.reshape(2, A, B, POL, BLOCKS * 8, LANES)
    flat = flat.swapaxes(3, 4).reshape(2, A, B, BLOCKS * 16, LANES)
    return pl.pallas_call(
        channelize_kernel,
        name="channelize",
        in_specs=[pl.BlockSpec(memory_space=pltpu.HBM)] * 4,
        out_shape=jax.ShapeDtypeStruct((128, B, 2, 16, LANES), BF16),
        scratch_shapes=[
            pltpu.VMEM((B, 2, A, BLOCKS * 16, LANES), BF16),
            pltpu.VMEM((TAPS, NCHAN), F32),
            pltpu.VMEM((256, 256), BF16),
            pltpu.VMEM((16, LANES), F32),
            pltpu.VMEM((TAPS * 16, LANES), F32),
            pltpu.VMEM((TAPS * 16, LANES), BF16),
            pltpu.VMEM((2, 2, FRAMES * 16, LANES), F32),
            pltpu.VMEM((B * A, 256, 256), BF16),
            pltpu.VMEM((2, 512 * A, LANES), F32),
            pltpu.SemaphoreType.DMA((B + 4,)),
        ],
        compiler_params=pltpu.CompilerParams(vmem_limit_bytes=40 << 20),
    )(in_hbm(flat), in_hbm(fir), in_hbm(jnp.asarray(dft_table())), in_hbm(jnp.asarray(twiddle_table())))


def beam_kernel(in_ref, row_ref, col_ref, sum_ref, out_ref, turn):
    def row_step(high, carry):
        for low in range(8):
            piece = jnp.concatenate(
                [in_ref[:, 2 * high + low // B, low % B, h].reshape(128, LANES) for h in range(2)], axis=1
            )
            got = jnp.dot(row_ref[...], piece, preferred_element_type=F32)
            for h in range(2):
                turn[h, pl.ds((2 * high + low // B) * 512 + low % B, 128, stride=4), :] = got[:, h * LANES:(h + 1) * LANES]
        return carry

    lax.fori_loop(0, NCOL // 8, row_step, 0, unroll=8)

    def col_step(g, carry):
        pows = []
        for j in range(4):
            base = (4 * g + j) * 8
            mids = []
            for h in range(2):
                rows = [turn[h, pl.ds(pl.multiple_of(c * 512 + base, 8), 8), :] for c in range(COLS)]
                mids.append(jnp.concatenate(rows, axis=0).astype(BF16))
            beam = jnp.dot(col_ref[...], jnp.concatenate(mids, axis=1), preferred_element_type=F32)
            re = beam[:NCOL]
            im = beam[NCOL:]
            pows.append((re * re + im * im).astype(BF16))
        power = jnp.concatenate(pows, axis=0)
        out_ref[g] = lax.dot_general(
            sum_ref[...], power, (((1,), (1,)), ((), ())), preferred_element_type=F32
        ).astype(BF16)
        return carry

    lax.fori_loop(0, COLS, col_step, 0, unroll=16)


def beamform(got):
    return pl.pallas_call(
        beam_kernel,
        name="beamform",
        out_shape=jax.ShapeDtypeStruct((COLS, 16, 256), BF16),
        scratch_shapes=[pltpu.VMEM((2, 128 * NCOL, LANES), F32)],
        compiler_params=pltpu.CompilerParams(vmem_limit_bytes=40 << 20),
    )(
        got.reshape(ROWS, COLS, B, 2, 16, LANES),
        jnp.asarray(row_matrix()),
        jnp.asarray(col_matrix()),
        jnp.asarray(sum_matrix()),
    )


def finish_kernel(in_ref, out_ref):
    wide = in_ref[...].astype(F32)
    for p in range(POL):
        piece = wide[:, p * 8:(p + 1) * 8, :].reshape(128, 256)
        out_ref[pl.ds(p, 256, stride=2), :] = piece.T


def finish(got):
    return pl.pallas_call(
        finish_kernel,
        name="finish",
        in_specs=[pl.BlockSpec(memory_space=pltpu.VMEM)],
        out_shape=jax.ShapeDtypeStruct((256 * POL, LANES), F32),
    )(pltpu.with_memory_space_constraint(got, pltpu.VMEM))


def body(volts, fir):
    spectra = channelize(volts, fir)
    gathered = lax.all_to_all(spectra, ("row", "col"), 0, 0, tiled=True)
    partial = beamform(gathered)
    swapped = lax.all_to_all(partial, "col", 0, 0, tiled=True)
    return finish(swapped).reshape(NROW // COLS, NCOL, POL, LANES)


def solution(mesh):
    in_specs = (P(None, "row", "col", None, None), P())
    out_specs = P("col", None, None, "row")
    return jax.shard_map(body, mesh=mesh, in_specs=in_specs, out_specs=out_specs, check_vma=False)
```

```python
import functools

import math

import jax
import jax.numpy as jnp
import numpy as np
from jax import lax
from jax.experimental import pallas as pl
from jax.experimental.pallas import tpu as pltpu
from jax.sharding import PartitionSpec as P

NROW = 64
NCOL = 64
POL = 2
NCHAN = 1024
TAPS = 16
FRAMES = 16
ROWS = 8
COLS = 16
A = NROW // ROWS
B = NCOL // COLS
BLOCKS = FRAMES + TAPS - 1
LANES = 128
GROUP = 16
F32 = jnp.float32
BF16 = jnp.bfloat16


def bf16_pair(angle):
    cosine = np.cos(angle).astype(np.float32).astype(jnp.bfloat16)
    sine = np.sin(angle).astype(np.float32).astype(jnp.bfloat16)
    return cosine, sine


def complex_table(angle):
    cosine, sine = bf16_pair(angle)
    real = np.stack([cosine, sine], axis=-1)
    imag = np.stack([-sine, cosine], axis=-1)
    return np.stack([real, imag], axis=1)


def dft_table():
    k = np.arange(LANES)
    table = complex_table(2.0 * np.pi * (np.outer(k, k) % LANES) / LANES)
    return table.transpose(0, 1, 3, 2).reshape(2 * LANES, 2 * LANES)


def twiddle_table():
    angle = 2.0 * np.pi * np.outer(np.arange(8), np.arange(LANES)) / NCHAN
    return np.concatenate([np.cos(angle), np.sin(angle)]).astype(np.float32)


def spatial(length):
    index = np.arange(length)
    return complex_table(2.0 * np.pi * (np.outer(index, index) % length) / length)


def row_matrix():
    table = spatial(NROW).reshape(NROW, 2, ROWS, A // 4, 4, 2)
    return table.transpose(0, 1, 2, 3, 5, 4).reshape(2 * NROW, 2 * NROW)


def col_matrix():
    table = spatial(NCOL).reshape(NCOL, 2, COLS, B, 2)
    return table.transpose(1, 0, 2, 4, 3).reshape(2 * NCOL, 2 * NCOL)


def sum_matrix():
    eye = np.eye(8, dtype=np.float32).reshape(2, 4, 2, 4)
    ones = np.ones(4, np.float32)
    full = np.einsum("hqHQ,pP,g,f->phqHQgPf", eye, np.eye(2, dtype=np.float32), ones, ones)
    return (full.reshape(16, 256) / (FRAMES * NROW * NCOL)).astype(jnp.bfloat16)


def channelize_kernel(x_hbm, fir_hbm, dft_hbm, tw_hbm, out_ref, x_ref, fir_ref, dft_ref, tw_ref, coef, filt, zed, turn, sems):
    x_copies = [pltpu.make_async_copy(x_hbm.at[:, :, b], x_ref.at[b], sems.at[b]) for b in range(1, B)]
    head_copy = pltpu.make_async_copy(x_hbm.at[:, :2, 0], x_ref.at[0, :, :2], sems.at[0])
    tail_copy = pltpu.make_async_copy(x_hbm.at[:, 2:, 0], x_ref.at[0, :, 2:], sems.at[B + 3])
    fir_copy = pltpu.make_async_copy(fir_hbm, fir_ref, sems.at[B])
    dft_copy = pltpu.make_async_copy(dft_hbm, dft_ref, sems.at[B + 1])
    tw_copy = pltpu.make_async_copy(tw_hbm, tw_ref, sems.at[B + 2])
    fir_copy.start()
    head_copy.start()
    tail_copy.start()
    tw_copy.start()
    for copy in x_copies:
        copy.start()
    dft_copy.start()
    fir_copy.wait()
    for s in range(8):
        piece = fir_ref[:, s * LANES:(s + 1) * LANES]
        for p in range(POL):
            coef[pl.ds(2 * s + p, TAPS, stride=16), :] = piece

    def filter_pair(index, units=((0, 0), (0, 1), (1, 0), (1, 1))):
        col = index // (A // 2)
        pair = index % (A // 2)
        for which, part in units:
                taps = [coef[16 * t:16 * t + 16, :].astype(BF16) for t in range(TAPS)]
                xs = [x_ref[col, part, 2 * pair + which, 16 * i:16 * i + 16, :] for i in range(BLOCKS)]
                for f in range(FRAMES):
                    terms = [taps[t] * xs[f + t] for t in range(TAPS)]
                    while len(terms) > TAPS // GROUP:
                        terms = [a + b for a, b in zip(terms[::2], terms[1::2])]
                    terms = [t.astype(F32) for t in terms]
                    while len(terms) > 1:
                        terms = [a + b for a, b in zip(terms[::2], terms[1::2])]
                    row = (f // 4) * 64 + f % 4
                    filt[which, part, pl.ds(row, 16, stride=4), :] = terms[0]

    def load_rows(which, part, t, j):
        lo = filt[which, part, 128 * t + 8 * j:128 * t + 8 * j + 8, :]
        hi = filt[which, part, 128 * t + 64 + 8 * j:128 * t + 64 + 8 * j + 8, :]
        return jnp.concatenate([lo, hi], axis=0)

    def dft4(y):
        (r0, i0), (r1, i1), (r2, i2), (r3, i3) = y
        sr0, si0 = r0 + r2, i0 + i2
        sr1, si1 = r1 + r3, i1 + i3
        dr0, di0 = r0 - r2, i0 - i2
        dr1, di1 = r1 - r3, i1 - i3
        return [
            (sr0 + sr1, si0 + si1),
            (dr0 + di1, di0 - dr1),
            (sr0 - sr1, si0 - si1),
            (dr0 - di1, di0 + dr1),
        ]

    def butterfly(slot):
        half = math.sqrt(0.5)
        for which in range(2):
            for t in range(2):
                re = [load_rows(which, 0, t, j) for j in range(8)]
                im = [load_rows(which, 1, t, j) for j in range(8)]
                sums = [(re[j] + re[j + 4], im[j] + im[j + 4]) for j in range(4)]
                (r0, i0), (r1, i1), (r2, i2), (r3, i3) = [
                    (re[j] - re[j + 4], im[j] - im[j + 4]) for j in range(4)
                ]
                odds = [
                    (r0, i0),
                    ((r1 + i1) * half, (i1 - r1) * half),
                    (i2, -r2),
                    ((i3 - r3) * half, (r3 + i3) * -half),
                ]
                for parity, outs in enumerate((dft4(sums), dft4(odds))):
                    for r in range(4):
                        q = 2 * r + parity
                        zr, zi = outs[r]
                        if q > 0:
                            cosine = tw_ref[q:q + 1, :]
                            sine = tw_ref[8 + q:9 + q, :]
                            zr, zi = zr * cosine + zi * sine, zi * cosine - zr * sine
                        row = q * 32 + t * 16
                        zed[2 * slot + which, row:row + 16, :LANES] = zr.astype(BF16)
                        zed[2 * slot + which, row:row + 16, LANES:] = zi.astype(BF16)

    head_copy.wait()
    filter_pair(0)
    tw_copy.wait()
    tail_copy.wait()

    def pair_step(index, carry):
        col = (index + 1) // (A // 2)

        @pl.when(index % (A // 2) == A // 2 - 1)
        def _():
            pltpu.make_async_copy(x_hbm.at[:, :, col], x_ref.at[col], sems.at[col]).wait()

        butterfly(index)
        filter_pair(index + 1)
        return carry

    lax.fori_loop(0, B * A // 2 - 1, pair_step, 0)
    butterfly(B * A // 2 - 1)
    dft_copy.wait()

    def transform_step(col, carry):
        for ant in range(A):
            spec = lax.dot_general(
                dft_ref[...], zed[col * A + ant], (((1,), (1,)), ((), ())), preferred_element_type=F32
            )
            for h in range(2):
                row = (2 * h + ant // 4) * 1024 + ant % 4
                turn[col % 2, pl.ds(row, 256, stride=4), :] = spec[:, h * LANES:(h + 1) * LANES]
        for h in range(2):
            rows = [turn[col % 2, i * 1024:(i + 1) * 1024, :].reshape(128, 8, LANES) for i in (2 * h, 2 * h + 1)]
            out_ref[:, col, h] = jnp.concatenate(rows, axis=1).astype(BF16)
        return carry

    for col in range(B):
        transform_step(col, 0)


def in_hbm(x):
    return pltpu.with_memory_space_constraint(x, pltpu.HBM)


def channelize(volts, fir):
    flat = volts.reshape(2, A, B, POL, BLOCKS * 8, LANES)
    flat = flat.swapaxes(3, 4).reshape(2, A, B, BLOCKS * 16, LANES)
    return pl.pallas_call(
        channelize_kernel,
        name="channelize",
        in_specs=[pl.BlockSpec(memory_space=pltpu.HBM)] * 4,
        out_shape=jax.ShapeDtypeStruct((128, B, 2, 16, LANES), BF16),
        scratch_shapes=[
            pltpu.VMEM((B, 2, A, BLOCKS * 16, LANES), BF16),
            pltpu.VMEM((TAPS, NCHAN), F32),
            pltpu.VMEM((256, 256), BF16),
            pltpu.VMEM((16, LANES), F32),
            pltpu.VMEM((TAPS * 16, LANES), F32),
            pltpu.VMEM((2, 2, FRAMES * 16, LANES), F32),
            pltpu.VMEM((B * A, 256, 256), BF16),
            pltpu.VMEM((2, 512 * A, LANES), F32),
            pltpu.SemaphoreType.DMA((B + 4,)),
        ],
        compiler_params=pltpu.CompilerParams(vmem_limit_bytes=40 << 20),
    )(in_hbm(flat), in_hbm(fir), in_hbm(jnp.asarray(dft_table())), in_hbm(jnp.asarray(twiddle_table())))


def beam_kernel(in_ref, row_ref, col_ref, sum_ref, out_ref, turn, pows_ref):
    def row_step(high, carry):
        for low in range(8):
            piece = jnp.concatenate(
                [in_ref[:, 2 * high + low // B, low % B, h].reshape(128, LANES) for h in range(2)], axis=1
            )
            got = jnp.dot(row_ref[...], piece, preferred_element_type=F32)
            for h in range(2):
                turn[h, pl.ds((2 * high + low // B) * 512 + low % B, 128, stride=4), :] = got[:, h * LANES:(h + 1) * LANES]
        return carry

    lax.fori_loop(0, NCOL // 8, row_step, 0, unroll=8)

    def col_step(g, carry):
        pows = []
        for j in range(4):
            base = (4 * g + j) * 8
            mids = []
            for h in range(2):
                rows = [turn[h, pl.ds(pl.multiple_of(c * 512 + base, 8), 8), :] for c in range(COLS)]
                mids.append(jnp.concatenate(rows, axis=0).astype(BF16))
            beam = jnp.dot(col_ref[...], jnp.concatenate(mids, axis=1), preferred_element_type=F32)
            re = beam[:NCOL]
            im = beam[NCOL:]
            pows.append((re * re + im * im).astype(BF16))
        pows_ref[g] = jnp.concatenate(pows, axis=0)
        return carry

    lax.fori_loop(0, COLS, col_step, 0, unroll=16)

    for g in range(COLS):
        out_ref[g] = lax.dot_general(
            sum_ref[...], pows_ref[g], (((1,), (1,)), ((), ())), preferred_element_type=F32
        ).astype(BF16)


def beamform(got):
    return pl.pallas_call(
        beam_kernel,
        name="beamform",
        out_shape=jax.ShapeDtypeStruct((COLS, 16, 256), BF16),
        scratch_shapes=[pltpu.VMEM((2, 128 * NCOL, LANES), F32), pltpu.VMEM((COLS, 256, 256), BF16)],
        compiler_params=pltpu.CompilerParams(vmem_limit_bytes=40 << 20),
    )(
        got.reshape(ROWS, COLS, B, 2, 16, LANES),
        jnp.asarray(row_matrix()),
        jnp.asarray(col_matrix()),
        jnp.asarray(sum_matrix()),
    )


def finish_kernel(in_ref, out_ref):
    wide = in_ref[...].astype(F32)
    for p in range(POL):
        piece = wide[:, p * 8:(p + 1) * 8, :].reshape(128, 256)
        out_ref[pl.ds(p, 256, stride=2), :] = piece.T


def finish(got):
    return pl.pallas_call(
        finish_kernel,
        name="finish",
        in_specs=[pl.BlockSpec(memory_space=pltpu.VMEM)],
        out_shape=jax.ShapeDtypeStruct((256 * POL, LANES), F32),
    )(pltpu.with_memory_space_constraint(got, pltpu.VMEM))


def body(volts, fir):
    spectra = channelize(volts, fir)
    gathered = lax.all_to_all(spectra, ("row", "col"), 0, 0, tiled=True)
    partial = beamform(gathered)
    swapped = lax.all_to_all(partial, "col", 0, 0, tiled=True)
    return finish(swapped).reshape(NROW // COLS, NCOL, POL, LANES)


def solution(mesh):
    in_specs = (P(None, "row", "col", None, None), P())
    out_specs = P("col", None, None, "row")
    return jax.shard_map(body, mesh=mesh, in_specs=in_specs, out_specs=out_specs, check_vma=False)
```
